32 devices in a mesh: trow: 4 (over y, x), tcol: 4 (over z), tm: 2 (over core).
Axes of the slice: x: 2, y: 2, z: 4, core: 2. Of those that a mesh axis runs over, the one named last changes fastest.
Arguments:
- start_field: float32 [2, 2, 8, 4096], P('tm', None, None, 'tcol'), may hold values from -6 to 6
- u_tiles: bfloat16 [2, 2, 4096, 2048], P('tm', None, 'trow', 'tcol'), may hold values from -0.25 to 0.25
- v_tiles: bfloat16 [2, 2, 2048, 4096], P('tm', None, 'trow', 'tcol'), may hold values from -0.0546875 to 0.0546875
- rank_blocks: int32 [2, 4, 4], P('tm', 'trow', 'tcol'), may hold values from 1 to 2
- onset_receiver: int32 [8, 4096], P(None, 'trow'), may hold values from 128 to 1023
- onset_source: int32 [8, 4096], P(None, 'tcol'), may hold values from 128 to 1023
- omega: float32 [2], replicated, may hold values from 0.1 to 0.9
Outputs:
- plus_field: float32 [2, 2, 8, 4096], P('tm', None, None, 'tcol')
- minus_field: bfloat16 [2, 2, 8, 4096], P('tm', None, None, 'trow')
The draws below stay inside these ranges and needn't reach their ends.
Inputs may be any that keep to these rules, and one draw needn't show every extreme that they name: `rank_blocks`: tiles use whole rank blocks; a tile with the most uses all 512 columns.
All inputs are finite; a program needn't handle non-finite values.
Results may differ from the reference program's by a relative error of at most 0.01.
Values may be sent and summed in bfloat16 or wider, within the bound.
A program may use at most 64 MiB of HBM per device.

```python
import jax
import jax.numpy as jnp
from jax import lax

TILE = 1024
RBLK = 256
RBMAX = 2
RMAX = 512
NV = 8
NT = 1024
ITERS = 1
NFQ = 2
NR = 4096
NS = 4096
N_TROW = 4
N_TCOL = 4


def with_ends(result, own_key, least, high):
    dims = result.shape
    spot = [jax.random.randint(jax.random.fold_in(own_key, axis), (), 0, dims[axis]) for axis in range(len(dims))]
    result = result.at[tuple(spot)].set(least)
    longest = dims.index(max(dims))
    spot[longest] = (spot[longest] + 1) % dims[longest]
    return result.at[tuple(spot)].set(high)


def block_scale(rng, shape, cuts, low, top_value):
    def one(axis_at, parts):
        heights = jax.random.uniform(jax.random.fold_in(jax.random.fold_in(rng, 6), axis_at), (parts,), jnp.float32, low / len(cuts), top_value / len(cuts))
        return jnp.repeat(jnp.exp(heights), shape[axis_at] // parts).reshape((-1,) + (1,) * (len(shape) - axis_at - 1))

    factor_of = one(*cuts[0])
    for cut in cuts[1:]:
        factor_of = factor_of * one(*cut)
    return factor_of


def bell_draw(own_key, shape, deviation, reach, split=(), kind=jnp.bfloat16):
    drawn = deviation * jax.random.normal(own_key, shape, jnp.float32)
    if split:
        drawn = drawn * block_scale(own_key, shape, split, -0.22, 0.18)
    return jnp.clip(drawn, -reach, reach).astype(kind)


def setup_inputs(seed: int = 0) -> dict:
    streams_of = jax.random.split(jax.random.key(seed), 8)
    start_field = bell_draw(streams_of[0], (NFQ, 2, NV, NS), 1.0, 6.0, ((0, 2), (3, 4)), jnp.float32)
    u_tiles = bell_draw(streams_of[1], (NFQ, 2, NR, N_TCOL * RMAX), RMAX ** -0.5, 0.25, ((0, 2), (2, 4), (3, 4)))
    v_tiles = bell_draw(streams_of[2], (NFQ, 2, N_TROW * RMAX, NS), ((4 * (NR + NS)) // 3) ** -0.5, 0.0546875, ((0, 2), (2, 4), (3, 4)))
    rank_blocks = with_ends(jax.random.randint(streams_of[3], (NFQ, N_TROW, N_TCOL), 1, RBMAX + 1), jax.random.fold_in(streams_of[3], 1), 1, RBMAX).astype(jnp.int32)
    onset_receiver = with_ends(jax.random.randint(streams_of[4], (NV, NR), NT // 8, NT), jax.random.fold_in(streams_of[4], 1), NT // 8, NT - 1).astype(jnp.int32)
    onset_source = with_ends(jax.random.randint(streams_of[5], (NV, NS), NT // 8, NT), jax.random.fold_in(streams_of[5], 1), NT // 8, NT - 1).astype(jnp.int32)
    omega = jnp.clip(jax.random.uniform(streams_of[6], (NFQ,), jnp.float32, 0.1, 0.9), 0.1, 0.9)
    return dict(start_field=start_field, u_tiles=u_tiles, v_tiles=v_tiles, rank_blocks=rank_blocks, onset_receiver=onset_receiver, onset_source=onset_source, omega=omega)


HIGHEST = lax.Precision.HIGHEST


def rounded(array_value):
    return lax.optimization_barrier(array_value.astype(jnp.bfloat16)).astype(jnp.float32)


def product(form, left_side, right_side):
    return jnp.einsum(form, left_side, right_side, precision=HIGHEST)


def window_field(field, onset, omega):
    time_grid = jnp.arange(NT, dtype=jnp.float32)
    time_index = jnp.arange(NT, dtype=jnp.int32)
    phase_grid = omega[:, None] * time_grid[None, :]
    cosine = jnp.cos(phase_grid)
    sine_table = jnp.sin(phase_grid)
    synth_basis = jnp.stack([cosine, -sine_table], axis=1).reshape(2 * NFQ, NT)
    by_point = jnp.transpose(field, (2, 0, 1, 3))

    def per_point(point_pair):
        field_part, limits = point_pair
        coefficients = field_part.reshape(2 * NFQ, field_part.shape[-1])
        traces = jnp.dot(coefficients.T, synth_basis, precision=HIGHEST, preferred_element_type=jnp.float32)
        keep_mask = time_index[None, :] < limits[:, None]
        traces = jnp.where(keep_mask, traces, jnp.zeros_like(traces))
        real_part = jnp.dot(traces, cosine.T, precision=HIGHEST, preferred_element_type=jnp.float32) * (2.0 / NT)
        imag_part = -jnp.dot(traces, sine_table.T, precision=HIGHEST, preferred_element_type=jnp.float32) * (2.0 / NT)
        return jnp.stack([real_part.T, imag_part.T], axis=1)

    windowed = lax.map(per_point, (by_point, onset))
    return jnp.transpose(windowed, (1, 2, 0, 3))


def row_factors(u_tiles, v_tiles, rank_blocks, row_index):
    u_rows = lax.dynamic_slice_in_dim(u_tiles, row_index * TILE, TILE, axis=2).astype(jnp.float32)
    u_rows = u_rows.reshape(NFQ, 2, TILE, N_TCOL, RMAX)
    v_rows = lax.dynamic_slice_in_dim(v_tiles, row_index * RMAX, RMAX, axis=2).astype(jnp.float32)
    v_rows = v_rows.reshape(NFQ, 2, RMAX, N_TCOL, TILE)
    blocks = lax.dynamic_index_in_dim(rank_blocks, row_index, axis=1, keepdims=False)
    rank_index = jnp.arange(RMAX, dtype=jnp.int32)
    live_mask = (rank_index[None, None, :] < blocks[:, :, None] * RBLK).astype(jnp.float32)
    return u_rows, v_rows, live_mask[:, None]


def forward_apply(field, u_tiles, v_tiles, rank_blocks):
    field_in = rounded(field).reshape(NFQ, 2, NV, N_TCOL, TILE)

    def one_row(row_index):
        u_rows, v_rows, live_mask = row_factors(u_tiles, v_tiles, rank_blocks, row_index)
        form = 'kvbj,krbj->kvbr'
        t_real = product(form, field_in[:, 0], v_rows[:, 0]) - product(form, field_in[:, 1], v_rows[:, 1])
        t_imag = product(form, field_in[:, 0], v_rows[:, 1]) + product(form, field_in[:, 1], v_rows[:, 0])
        t_real = rounded(t_real * live_mask)
        t_imag = rounded(t_imag * live_mask)
        back = 'kibr,kvbr->kvi'
        y_real = product(back, u_rows[:, 0], t_real) - product(back, u_rows[:, 1], t_imag)
        y_imag = product(back, u_rows[:, 0], t_imag) + product(back, u_rows[:, 1], t_real)
        return jnp.stack([y_real, y_imag], axis=1)

    rows_out = lax.map(one_row, jnp.arange(N_TROW, dtype=jnp.int32))
    return jnp.transpose(rows_out, (1, 2, 3, 0, 4)).reshape(NFQ, 2, NV, NR)


def adjoint_apply(field, u_tiles, v_tiles, rank_blocks):
    field_in = rounded(field).reshape(NFQ, 2, NV, N_TROW, TILE)

    def one_row(total, row_index):
        u_rows, v_rows, live_mask = row_factors(u_tiles, v_tiles, rank_blocks, row_index)
        row_field = lax.dynamic_index_in_dim(field_in, row_index, axis=3, keepdims=False)
        form = 'kvi,kibr->kvbr'
        s_real = product(form, row_field[:, 0], u_rows[:, 0]) + product(form, row_field[:, 1], u_rows[:, 1])
        s_imag = product(form, row_field[:, 1], u_rows[:, 0]) - product(form, row_field[:, 0], u_rows[:, 1])
        s_real = rounded(s_real * live_mask)
        s_imag = rounded(s_imag * live_mask)
        back = 'kvbr,krbj->kvbj'
        x_real = product(back, s_real, v_rows[:, 0]) + product(back, s_imag, v_rows[:, 1])
        x_imag = product(back, s_imag, v_rows[:, 0]) - product(back, s_real, v_rows[:, 1])
        return total + jnp.stack([x_real, x_imag], axis=1), None

    start_total = jnp.zeros((NFQ, 2, NV, N_TCOL, TILE), jnp.float32)
    total, unused = lax.scan(one_row, start_total, jnp.arange(N_TROW, dtype=jnp.int32))
    return total.reshape(NFQ, 2, NV, NS)


def reference(start_field, u_tiles, v_tiles, rank_blocks, onset_receiver, onset_source, omega):
    plus_field = start_field
    minus_field = jnp.zeros((NFQ, 2, NV, NR), jnp.float32)
    for iteration in range(ITERS):
        minus_field = rounded(window_field(forward_apply(plus_field, u_tiles, v_tiles, rank_blocks), onset_receiver, omega))
        plus_field = start_field - window_field(adjoint_apply(minus_field, u_tiles, v_tiles, rank_blocks), onset_source, omega)
    return plus_field, minus_field.astype(jnp.bfloat16)
```

```python
import functools

import jax
import jax.numpy as jnp
from jax import lax
from jax.experimental import pallas as pl
from jax.experimental.pallas import tpu as pltpu
from jax.sharding import PartitionSpec as P

RBLK = 256
NT = 1024
MESH = pl.DeviceIdType.MESH
F32 = jnp.float32
BF16 = jnp.bfloat16


def contract_last(left_side, right_side):
    return lax.dot_general(
        left_side, right_side, (((1,), (1,)), ((), ())), preferred_element_type=F32
    )


def contract_inner(left_side, right_side):
    return lax.dot_general(
        left_side, right_side, (((1,), (0,)), ((), ())), preferred_element_type=F32
    )


def sin_cos(angle):
    turns = jnp.floor(angle * 0.6366197723675814 + 0.5)
    rest = angle - turns * 1.5703125
    rest = rest - turns * 4.837512969970703e-4
    rest = rest - turns * 7.549789948768648e-8
    square = rest * rest
    sine = rest + rest * square * (
        -1.6666654611e-1 + square * (8.3321608736e-3 - square * 1.9515295891e-4)
    )
    cosine = 1.0 - 0.5 * square + square * square * (
        4.166664568298827e-2 + square * (-1.388731625493765e-3 + square * 2.443315711809948e-5)
    )
    quarter = turns - 4.0 * jnp.floor(turns * 0.25)
    swap = (quarter == 1.0) | (quarter == 3.0)
    first = jnp.where(swap, cosine, sine)
    second = jnp.where(swap, sine, cosine)
    first = jnp.where(quarter >= 2.0, -first, first)
    second = jnp.where((quarter == 1.0) | (quarter == 2.0), -second, second)
    return first, second


def prefix_sums(phi, count):
    sine, cosine = sin_cos(phi)
    sine_n, cosine_n = sin_cos(count * phi)
    still = phi == 0.0
    ratio = jnp.where(still, count, sine_n / jnp.where(still, 1.0, sine))
    cos_sum = ratio * (cosine_n * cosine + sine_n * sine)
    sin_sum = ratio * (sine_n * cosine - cosine_n * sine)
    return cos_sum, sin_sum


def gram(onset, omega_a, omega_b):
    count = onset.astype(F32)
    omega_a = jnp.full(count.shape, omega_a, F32)
    omega_b = jnp.full(count.shape, omega_b, F32)
    cos_aa, sin_aa = prefix_sums(omega_a, count)
    cos_bb, sin_bb = prefix_sums(omega_b, count)
    cos_sum, sin_sum = prefix_sums(0.5 * (omega_a + omega_b), count)
    cos_dif, sin_dif = prefix_sums(0.5 * (omega_a - omega_b), count)
    scale = 1.0 / NT
    g = {}
    g[0, 0] = scale * (count + cos_aa)
    g[1, 1] = scale * (count - cos_aa)
    g[0, 1] = -scale * sin_aa
    g[2, 2] = scale * (count + cos_bb)
    g[3, 3] = scale * (count - cos_bb)
    g[2, 3] = -scale * sin_bb
    g[0, 2] = scale * (cos_dif + cos_sum)
    g[1, 3] = scale * (cos_dif - cos_sum)
    g[0, 3] = -scale * (sin_sum - sin_dif)
    g[1, 2] = -scale * (sin_sum + sin_dif)
    for m in range(4):
        for n in range(m):
            g[m, n] = g[n, m]
    return g


def apply_gram(g, y):
    return [
        g[m, 0] * y[0] + g[m, 1] * y[1] + g[m, 2] * y[2] + g[m, 3] * y[3] for m in range(4)
    ]


def kernel(
    n_row, n_col, direct_onset,
    start_hbm, u_hbm, v_hbm, rank_ref, onset_r_hbm, onset_s_hbm, omega_ref,
    plus_ref, minus_ref,
    start_buf, u_buf, v_buf, onset_buf, local_sem,
    send1, recv1, send2, recv2, send3, recv3, send4, recv4,
    ssem1, rsem1, ssem2, rsem2, ssem3, rsem3, ssem4, rsem4,
):
    row = lax.axis_index("trow")
    col = lax.axis_index("tcol")
    freq = lax.axis_index("tm")
    group_r, group_s = 2 * n_col, 2 * n_row
    me_r = col * 2 + freq
    me_s = row * 2 + freq
    width_r = recv1.shape[2]
    width_s = recv3.shape[2]

    def peer_r(index):
        return {"tcol": index // 2, "tm": index % 2}

    def peer_s(index):
        return {"trow": index // 2, "tm": index % 2}

    barrier = pltpu.get_barrier_semaphore()
    for step in range(1, group_r):
        pl.semaphore_signal(
            barrier, inc=1, device_id=peer_r((me_r + step) % group_r), device_id_type=MESH
        )
    for step in range(1, group_s):
        pl.semaphore_signal(
            barrier, inc=1, device_id=peer_s((me_s + step) % group_s), device_id_type=MESH
        )

    def onset_src(hbm, me, width):
        if direct_onset:
            return hbm.at[:, pl.ds(pl.multiple_of(me * width, width), width)]
        return hbm.at[me]

    copies = [
        pltpu.make_async_copy(start_hbm.at[0], start_buf, local_sem.at[0]),
        pltpu.make_async_copy(v_hbm.at[0, 0], v_buf.at[0], local_sem.at[1]),
        pltpu.make_async_copy(v_hbm.at[0, 1], v_buf.at[1], local_sem.at[2]),
        pltpu.make_async_copy(u_hbm.at[0, 0], u_buf.at[0], local_sem.at[3]),
        pltpu.make_async_copy(u_hbm.at[0, 1], u_buf.at[1], local_sem.at[4]),
        pltpu.make_async_copy(
            onset_src(onset_r_hbm, me_r, width_r), onset_buf.at[0, :, pl.ds(0, width_r)], local_sem.at[5]
        ),
        pltpu.make_async_copy(
            onset_src(onset_s_hbm, me_s, width_s), onset_buf.at[1, :, pl.ds(0, width_s)], local_sem.at[6]
        ),
    ]
    for copy in copies:
        copy.start()

    def exchange(send_of, recv, ssem, rsem, me, group, peer):
        out = []
        for step in range(1, group):
            index = (me + step) % group
            copy = pltpu.make_async_remote_copy(
                src_ref=send_of(index),
                dst_ref=recv.at[me],
                send_sem=ssem.at[step],
                recv_sem=rsem.at[step],
                device_id=peer(index),
                device_id_type=MESH,
            )
            copy.start()
            out.append(copy)
        return out

    def arrivals(send_of, recv, ssem, rsem, me, group, peer):
        for step in range(1, group):
            index = (me + group - step) % group
            pltpu.make_async_remote_copy(
                src_ref=send_of(index),
                dst_ref=recv.at[index],
                send_sem=ssem.at[step],
                recv_sem=rsem.at[step],
                device_id=peer(index),
                device_id_type=MESH,
            ).wait_recv()

    def window(recv, group, onset, send):
        parts = []
        for k in range(2):
            total = recv[k].astype(F32)
            for other in range(1, group // 2):
                total = total + recv[2 * other + k].astype(F32)
            parts += [total[:8], total[8:]]
        done = apply_gram(onset, parts)
        for k in range(2):
            send[k] = jnp.concatenate([done[2 * k], done[2 * k + 1]], axis=0).astype(BF16)

    def live(width):
        lane = lax.broadcasted_iota(jnp.int32, (8, width), 1)
        return lane < rank_ref[0, 0, 0] * RBLK

    copies[0].wait()
    rows_in = jnp.concatenate([start_buf[0], start_buf[1]], axis=0).astype(BF16)
    copies[1].wait()
    first_real = contract_last(rows_in, v_buf[0])
    copies[2].wait()
    first_imag = contract_last(rows_in, v_buf[1])
    keep = live(first_real.shape[1])
    t_real = jnp.where(keep, first_real[:8] - first_imag[8:], 0.0)
    t_imag = jnp.where(keep, first_imag[:8] + first_real[8:], 0.0)
    packed = jnp.concatenate([t_real, t_imag], axis=0).astype(BF16)
    copies[3].wait()
    second_real = contract_last(packed, u_buf[0])
    copies[4].wait()
    second_imag = contract_last(packed, u_buf[1])
    field = jnp.concatenate(
        [second_real[:8] - second_imag[8:], second_imag[:8] + second_real[8:]], axis=0
    ).astype(BF16)
    for index in range(group_r):
        send1[index] = field[:, index * width_r : (index + 1) * width_r]
    recv1[me_r] = send1[me_r]
    pl.semaphore_wait(barrier, group_r + group_s - 2)

    of1 = lambda index: send1.at[index]
    of2 = lambda index: send2.at[index % 2]
    of3 = lambda index: send3.at[index]
    of4 = lambda index: send4.at[index % 2]
    sent = exchange(of1, recv1, ssem1, rsem1, me_r, group_r, peer_r)

    copies[5].wait()
    copies[6].wait()
    omega_a, omega_b = omega_ref[0], omega_ref[1]
    gram_r = gram(onset_buf[0, :, :width_r], omega_a, omega_b)
    gram_s = gram(onset_buf[1, :, :width_s], omega_a, omega_b)

    arrivals(of1, recv1, ssem1, rsem1, me_r, group_r, peer_r)
    window(recv1, group_r, gram_r, send2)
    sent += exchange(of2, recv2, ssem2, rsem2, me_r, group_r, peer_r)
    recv2[me_r] = send2[freq]
    arrivals(of2, recv2, ssem2, rsem2, me_r, group_r, peer_r)
    rows_back = jnp.concatenate([recv2[index] for index in range(group_r)], axis=1)
    minus_ref[0, 0] = rows_back[:8]
    minus_ref[0, 1] = rows_back[8:]

    first_real = contract_inner(rows_back, u_buf[0])
    first_imag = contract_inner(rows_back, u_buf[1])
    s_real = jnp.where(keep, first_real[:8] + first_imag[8:], 0.0)
    s_imag = jnp.where(keep, first_real[8:] - first_imag[:8], 0.0)
    packed = jnp.concatenate([s_real, s_imag], axis=0).astype(BF16)
    second_real = contract_inner(packed, v_buf[0])
    second_imag = contract_inner(packed, v_buf[1])
    field = jnp.concatenate(
        [second_real[:8] + second_imag[8:], second_real[8:] - second_imag[:8]], axis=0
    ).astype(BF16)
    for index in range(group_s):
        send3[index] = field[:, index * width_s : (index + 1) * width_s]
    recv3[me_s] = send3[me_s]
    sent += exchange(of3, recv3, ssem3, rsem3, me_s, group_s, peer_s)
    arrivals(of3, recv3, ssem3, rsem3, me_s, group_s, peer_s)
    window(recv3, group_s, gram_s, send4)
    sent += exchange(of4, recv4, ssem4, rsem4, me_s, group_s, peer_s)
    recv4[me_s] = send4[freq]
    arrivals(of4, recv4, ssem4, rsem4, me_s, group_s, peer_s)
    back = jnp.concatenate([recv4[index] for index in range(group_s)], axis=1).astype(F32)
    plus_ref[0, 0] = start_buf[0] - back[:8]
    plus_ref[0, 1] = start_buf[1] - back[8:]
    for copy in sent:
        copy.wait_send()


def per_device(start_field, u_tiles, v_tiles, rank_blocks, onset_receiver, onset_source, omega):
    n_row = lax.axis_size("trow")
    n_col = lax.axis_size("tcol")
    group_r, group_s = 2 * n_col, 2 * n_row
    tile_r, tile_s = u_tiles.shape[2], v_tiles.shape[3]
    width_r, width_s = tile_r // group_r, tile_s // group_s
    direct = width_r % 128 == 0 and width_s % 128 == 0
    if not direct:
        onset_receiver = onset_receiver.reshape(8, group_r, width_r).transpose(1, 0, 2)
        onset_source = onset_source.reshape(8, group_s, width_s).transpose(1, 0, 2)
    hbm = pl.BlockSpec(memory_space=pl.ANY)
    smem = pl.BlockSpec(memory_space=pltpu.SMEM)
    vmem = pl.BlockSpec(memory_space=pltpu.VMEM)
    piece_r = lambda count: pltpu.VMEM((count, 16, width_r), BF16)
    piece_s = lambda count: pltpu.VMEM((count, 16, width_s), BF16)
    return pl.pallas_call(
        functools.partial(kernel, n_row, n_col, direct),
        out_shape=(
            jax.ShapeDtypeStruct(start_field.shape, F32),
            jax.ShapeDtypeStruct((1, 2, 8, tile_r), BF16),
        ),
        in_specs=[hbm, hbm, hbm, smem, hbm, hbm, smem],
        out_specs=(vmem, vmem),
        scratch_shapes=[
            pltpu.VMEM(start_field.shape[1:], F32),
            pltpu.VMEM(u_tiles.shape[1:], BF16),
            pltpu.VMEM(v_tiles.shape[1:], BF16),
            pltpu.VMEM((2, 8, max(width_r, width_s)), jnp.int32),
            pltpu.SemaphoreType.DMA((7,)),
            piece_r(group_r), piece_r(group_r), piece_r(2), piece_r(group_r),
            piece_s(group_s), piece_s(group_s), piece_s(2), piece_s(group_s),
        ]
        + [pltpu.SemaphoreType.DMA((group_r,))] * 4
        + [pltpu.SemaphoreType.DMA((group_s,))] * 4,
        compiler_params=pltpu.CompilerParams(
            collective_id=0, has_side_effects=True, vmem_limit_bytes=32 * 1024 * 1024
        ),
    )(start_field, u_tiles, v_tiles, rank_blocks, onset_receiver, onset_source, omega)


def solution(mesh):
    placed = (
        P("tm", None, None, "tcol"),
        P("tm", None, "trow", "tcol"),
        P("tm", None, "trow", "tcol"),
        P("tm", "trow", "tcol"),
        P(None, "trow"),
        P(None, "tcol"),
        P(),
    )
    return jax.shard_map(
        per_device,
        mesh=mesh,
        in_specs=placed,
        out_specs=(P("tm", None, None, "tcol"), P("tm", None, None, "trow")),
        check_vma=False,
    )
```

```python
import functools

import jax
import jax.numpy as jnp
from jax import lax
from jax.experimental import pallas as pl
from jax.experimental.pallas import tpu as pltpu
from jax.sharding import PartitionSpec as P

RBLK = 256
NT = 1024
MESH = pl.DeviceIdType.MESH
F32 = jnp.float32
BF16 = jnp.bfloat16


def contract_last(left_side, right_side):
    return lax.dot_general(
        left_side, right_side, (((1,), (1,)), ((), ())), preferred_element_type=F32
    )


def contract_inner(left_side, right_side):
    return lax.dot_general(
        left_side, right_side, (((1,), (0,)), ((), ())), preferred_element_type=F32
    )


def sin_cos(angle):
    turns = jnp.floor(angle * 0.6366197723675814 + 0.5)
    rest = angle - turns * 1.5703125
    rest = rest - turns * 4.837512969970703e-4
    rest = rest - turns * 7.549789948768648e-8
    square = rest * rest
    sine = rest + rest * square * (
        -1.6666654611e-1 + square * (8.3321608736e-3 - square * 1.9515295891e-4)
    )
    cosine = 1.0 - 0.5 * square + square * square * (
        4.166664568298827e-2 + square * (-1.388731625493765e-3 + square * 2.443315711809948e-5)
    )
    quarter = turns - 4.0 * jnp.floor(turns * 0.25)
    swap = (quarter == 1.0) | (quarter == 3.0)
    first = jnp.where(swap, cosine, sine)
    second = jnp.where(swap, sine, cosine)
    first = jnp.where(quarter >= 2.0, -first, first)
    second = jnp.where((quarter == 1.0) | (quarter == 2.0), -second, second)
    return first, second


def prefix_sums(phi, count):
    sine, cosine = sin_cos(phi)
    sine_n, cosine_n = sin_cos(count * phi)
    still = phi == 0.0
    ratio = jnp.where(still, count, sine_n / jnp.where(still, 1.0, sine))
    cos_sum = ratio * (cosine_n * cosine + sine_n * sine)
    sin_sum = ratio * (sine_n * cosine - cosine_n * sine)
    return cos_sum, sin_sum


def gram(onset, omega_a, omega_b):
    count = onset.astype(F32)
    omega_a = jnp.full(count.shape, omega_a, F32)
    omega_b = jnp.full(count.shape, omega_b, F32)
    cos_aa, sin_aa = prefix_sums(omega_a, count)
    cos_bb, sin_bb = prefix_sums(omega_b, count)
    cos_sum, sin_sum = prefix_sums(0.5 * (omega_a + omega_b), count)
    cos_dif, sin_dif = prefix_sums(0.5 * (omega_a - omega_b), count)
    scale = 1.0 / NT
    g = {}
    g[0, 0] = scale * (count + cos_aa)
    g[1, 1] = scale * (count - cos_aa)
    g[0, 1] = -scale * sin_aa
    g[2, 2] = scale * (count + cos_bb)
    g[3, 3] = scale * (count - cos_bb)
    g[2, 3] = -scale * sin_bb
    g[0, 2] = scale * (cos_dif + cos_sum)
    g[1, 3] = scale * (cos_dif - cos_sum)
    g[0, 3] = -scale * (sin_sum - sin_dif)
    g[1, 2] = -scale * (sin_sum + sin_dif)
    for m in range(4):
        for n in range(m):
            g[m, n] = g[n, m]
    return g


def apply_gram(g, y):
    return [
        g[m, 0] * y[0] + g[m, 1] * y[1] + g[m, 2] * y[2] + g[m, 3] * y[3] for m in range(4)
    ]


def kernel(
    n_row, n_col, direct_onset,
    start_hbm, u_hbm, v_hbm, rank_ref, onset_r_hbm, onset_s_hbm, omega_hbm,
    out_ref,
    start_buf, u_buf, v_buf, omega_ref, onset_r_buf, onset_s_buf, local_sem,
    send1, recv1, send2, recv2, send3, recv3, send4, recv4,
    ssem1, rsem1, ssem2, rsem2, ssem3, rsem3, ssem4, rsem4,
):
    row = lax.axis_index("trow")
    col = lax.axis_index("tcol")
    freq = lax.axis_index("tm")
    group_r, group_s = 2 * n_col, 2 * n_row
    me_r = col * 2 + freq
    me_s = row * 2 + freq
    width_r = recv1.shape[2]
    half_s = recv3.shape[2]
    half_r = u_buf.shape[1] // 2
    half_group = group_r // 2

    def peer_r(index):
        return {"tcol": index // 2, "tm": index % 2}

    def peer_s(index):
        return {"trow": index // 2, "tm": index % 2}

    far = 1 - me_r // half_group
    near = 1 - far
    far_rows = pl.ds(pl.multiple_of(far * half_r, half_r), half_r)
    near_rows = pl.ds(pl.multiple_of(near * half_r, half_r), half_r)
    if direct_onset:
        onset_r_src = onset_r_hbm.at[:, pl.ds(pl.multiple_of(me_r * width_r, width_r), width_r)]
    else:
        onset_r_src = onset_r_hbm.at[me_r]
    onset_s_src = onset_s_hbm.at[:, pl.ds(pl.multiple_of(freq * half_s, half_s), half_s)]
    moves = [
        (start_hbm.at[0], start_buf),
        (v_hbm.at[0, 0], v_buf.at[0]),
        (v_hbm.at[0, 1], v_buf.at[1]),
        (u_hbm.at[0, 0, far_rows], u_buf.at[0, far_rows]),
        (u_hbm.at[0, 1, far_rows], u_buf.at[1, far_rows]),
        (u_hbm.at[0, 0, near_rows], u_buf.at[0, near_rows]),
        (u_hbm.at[0, 1, near_rows], u_buf.at[1, near_rows]),
        (omega_hbm, omega_ref),
        (onset_r_src, onset_r_buf),
        (onset_s_src, onset_s_buf),
    ]
    copies = [
        pltpu.make_async_copy(source, target, local_sem.at[place])
        for place, (source, target) in enumerate(moves)
    ]
    for copy in copies:
        copy.start()

    barrier = pltpu.get_barrier_semaphore()
    for step in range(1, group_r):
        pl.semaphore_signal(
            barrier, inc=1, device_id=peer_r((me_r + step) % group_r), device_id_type=MESH
        )
    for step in range(1, group_s):
        pl.semaphore_signal(
            barrier, inc=1, device_id=peer_s((me_s + step) % group_s), device_id_type=MESH
        )

    def remote(source, target, ssem, rsem, device):
        return pltpu.make_async_remote_copy(
            src_ref=source, dst_ref=target, send_sem=ssem, recv_sem=rsem,
            device_id=device, device_id_type=MESH,
        )

    sent = []

    def push(send_of, recv, ssem, rsem, me, index, peer):
        copy = remote(send_of(index), recv.at[me], ssem.at[index], rsem.at[me], peer(index))
        copy.start()
        sent.append(copy)

    def arrivals(send_of, recv, ssem, rsem, me, group, peer):
        for step in range(1, group):
            index = (me + step) % group
            remote(
                send_of(index), recv.at[index], ssem.at[index], rsem.at[index], peer(index)
            ).wait_recv()

    def window(recv, group, onset):
        parts = []
        for k in range(2):
            total = recv[k].astype(F32)
            for other in range(1, group // 2):
                total = total + recv[2 * other + k].astype(F32)
            parts += [total[:8], total[8:]]
        done = apply_gram(onset, parts)
        return [
            jnp.concatenate([done[2 * k], done[2 * k + 1]], axis=0).astype(BF16)
            for k in range(2)
        ]

    of1 = lambda index: send1.at[index]
    of2 = lambda index: send2.at[index % 2]
    of3 = lambda index: send3.at[index % 2]

    copies[0].wait()
    rows_in = jnp.concatenate([start_buf[0], start_buf[1]], axis=0).astype(BF16)
    copies[1].wait()
    first_real = contract_last(rows_in, v_buf[0])
    copies[2].wait()
    first_imag = contract_last(rows_in, v_buf[1])
    lane = lax.broadcasted_iota(jnp.int32, (8, first_real.shape[1]), 1)
    keep = lane < rank_ref[0, 0, 0] * RBLK
    t_real = jnp.where(keep, first_real[:8] - first_imag[8:], 0.0)
    t_imag = jnp.where(keep, first_imag[:8] + first_real[8:], 0.0)
    packed = jnp.concatenate([t_real, t_imag], axis=0).astype(BF16)

    def forward_half(half, rows, real_copy, imag_copy):
        real_copy.wait()
        second_real = contract_last(packed, u_buf[0, rows])
        imag_copy.wait()
        second_imag = contract_last(packed, u_buf[1, rows])
        field = jnp.concatenate(
            [second_real[:8] - second_imag[8:], second_imag[:8] + second_real[8:]], axis=0
        ).astype(BF16)
        for place in range(half_group):
            send1[half * half_group + place] = field[:, place * width_r : (place + 1) * width_r]

    forward_half(far, far_rows, copies[3], copies[4])
    pl.semaphore_wait(barrier, group_r + group_s - 2)
    for place in range(half_group):
        push(of1, recv1, ssem1, rsem1, me_r, far * half_group + place, peer_r)
    forward_half(near, near_rows, copies[5], copies[6])
    for step in range(1, half_group):
        push(
            of1, recv1, ssem1, rsem1, me_r,
            near * half_group + (me_r + step) % half_group, peer_r,
        )
    recv1[me_r] = send1[me_r]
    for place in (7, 8, 9):
        copies[place].wait()
    gram_r = gram(onset_r_buf[...], omega_ref[0], omega_ref[1])

    arrivals(of1, recv1, ssem1, rsem1, me_r, group_r, peer_r)
    done = window(recv1, group_r, gram_r)
    for k in range(2):
        send2[k] = done[k]
    for step in range(1, group_r):
        push(of2, recv2, ssem2, rsem2, me_r, (me_r + step) % group_r, peer_r)
    recv2[me_r] = send2[freq]
    gram_s = gram(onset_s_buf[...], omega_ref[0], omega_ref[1])
    arrivals(of2, recv2, ssem2, rsem2, me_r, group_r, peer_r)
    rows_back = jnp.concatenate([recv2[index] for index in range(group_r)], axis=1)

    first_real = contract_inner(rows_back, u_buf[0])
    first_imag = contract_inner(rows_back, u_buf[1])
    s_real = jnp.where(keep, first_real[:8] + first_imag[8:], 0.0)
    s_imag = jnp.where(keep, first_real[8:] - first_imag[:8], 0.0)
    packed_back = jnp.concatenate([s_real, s_imag], axis=0).astype(BF16)
    for half in range(2):
        span = slice(half * half_s, (half + 1) * half_s)
        second_real = contract_inner(packed_back, v_buf[0, :, span])
        second_imag = contract_inner(packed_back, v_buf[1, :, span])
        send3[half] = jnp.concatenate(
            [second_real[:8] + second_imag[8:], second_real[8:] - second_imag[:8]], axis=0
        ).astype(BF16)
        for step in range(1, n_row):
            push(
                of3, recv3, ssem3, rsem3, me_s, ((row + step) % n_row) * 2 + half, peer_s
            )
    partner = me_s + 1 - 2 * freq
    push(of3, recv3, ssem3, rsem3, me_s, partner, peer_s)
    recv3[me_s] = send3[freq]
    out_ref[1, 0] = rows_back[:8]
    out_ref[1, 1] = rows_back[8:]
    arrivals(of3, recv3, ssem3, rsem3, me_s, group_s, peer_s)
    done = window(recv3, group_s, gram_s)
    for k in range(2):
        send4[k] = done[k]
    last = remote(send4.at[1 - freq], recv4.at[freq], ssem4, rsem4, {"tm": 1 - freq})
    last.start()
    recv4[freq] = send4[freq]
    remote(send4.at[freq], recv4.at[1 - freq], ssem4, rsem4, {"tm": 1 - freq}).wait_recv()
    back = jnp.concatenate([recv4[0], recv4[1]], axis=1)
    out_ref[0, 0] = back[:8]
    out_ref[0, 1] = back[8:]
    for copy in sent:
        copy.wait_send()
    last.wait_send()


def per_device(start_field, u_tiles, v_tiles, rank_blocks, onset_receiver, onset_source, omega):
    n_row = lax.axis_size("trow")
    n_col = lax.axis_size("tcol")
    group_r, group_s = 2 * n_col, 2 * n_row
    tile_r, tile_s = u_tiles.shape[2], v_tiles.shape[3]
    width_r, half_s = tile_r // group_r, tile_s // 2
    direct = width_r % 128 == 0
    if not direct:
        onset_receiver = onset_receiver.reshape(8, group_r, width_r).transpose(1, 0, 2)
    hbm = pl.BlockSpec(memory_space=pl.ANY)
    piece_r = lambda count: pltpu.VMEM((count, 16, width_r), BF16)
    piece_s = lambda count: pltpu.VMEM((count, 16, half_s), BF16)
    sems = pltpu.SemaphoreType.DMA
    fields = pl.pallas_call(
        functools.partial(kernel, n_row, n_col, direct),
        out_shape=jax.ShapeDtypeStruct((2, 2, 8, tile_r), BF16),
        in_specs=[hbm] * 3 + [pl.BlockSpec(memory_space=pltpu.SMEM)] + [hbm] * 3,
        out_specs=pl.BlockSpec(memory_space=pltpu.VMEM),
        scratch_shapes=[
            pltpu.VMEM(start_field.shape[1:], F32),
            pltpu.VMEM(u_tiles.shape[1:], BF16),
            pltpu.VMEM(v_tiles.shape[1:], BF16),
            pltpu.SMEM((2,), F32),
            pltpu.VMEM((8, width_r), jnp.int32),
            pltpu.VMEM((8, half_s), jnp.int32),
            sems((10,)),
            piece_r(group_r), piece_r(group_r), piece_r(2), piece_r(group_r),
            piece_s(2), piece_s(group_s), piece_s(2), piece_s(2),
        ]
        + [sems((group_r,))] * 4
        + [sems((group_s,))] * 2
        + [sems(())] * 2,
        compiler_params=pltpu.CompilerParams(
            collective_id=0, has_side_effects=True, vmem_limit_bytes=24 * 1024 * 1024
        ),
    )(
        pin(start_field), pin(u_tiles), pin(v_tiles), rank_blocks,
        pin(onset_receiver), pin(onset_source), pin(omega),
    )
    return start_field - fields[:1].astype(F32), fields[1:]


def pin(x):
    return pltpu.with_memory_space_constraint(x, pltpu.MemorySpace.HBM)


def solution(mesh):
    placed = (
        P("tm", None, None, "tcol"),
        P("tm", None, "trow", "tcol"),
        P("tm", None, "trow", "tcol"),
        P("tm", "trow", "tcol"),
        P(None, "trow"),
        P(None, "tcol"),
        P(),
    )
    return jax.shard_map(
        per_device,
        mesh=mesh,
        in_specs=placed,
        out_specs=(P("tm", None, None, "tcol"), P("tm", None, None, "trow")),
        check_vma=False,
    )
```

```python
import functools

import jax
import jax.numpy as jnp
from jax import lax
from jax.experimental import pallas as pl
from jax.experimental.pallas import tpu as pltpu
from jax.sharding import PartitionSpec as P

RBLK = 256
NT = 1024
MESH = pl.DeviceIdType.MESH
F32 = jnp.float32
BF16 = jnp.bfloat16


def contract_last(left_side, right_side):
    return lax.dot_general(
        left_side, right_side, (((1,), (1,)), ((), ())), preferred_element_type=F32
    )


def contract_inner(left_side, right_side):
    return lax.dot_general(
        left_side, right_side, (((1,), (0,)), ((), ())), preferred_element_type=F32
    )


def sin_cos(angle):
    turns = jnp.floor(angle * 0.6366197723675814 + 0.5)
    rest = angle - turns * 1.5703125
    rest = rest - turns * 4.837512969970703e-4
    rest = rest - turns * 7.549789948768648e-8
    square = rest * rest
    sine = rest + rest * square * (
        -1.6666654611e-1 + square * (8.3321608736e-3 - square * 1.9515295891e-4)
    )
    cosine = 1.0 - 0.5 * square + square * square * (
        4.166664568298827e-2 + square * (-1.388731625493765e-3 + square * 2.443315711809948e-5)
    )
    quarter = turns - 4.0 * jnp.floor(turns * 0.25)
    swap = (quarter == 1.0) | (quarter == 3.0)
    first = jnp.where(swap, cosine, sine)
    second = jnp.where(swap, sine, cosine)
    first = jnp.where(quarter >= 2.0, -first, first)
    second = jnp.where((quarter == 1.0) | (quarter == 2.0), -second, second)
    return first, second


def prefix_sums(phi, count):
    sine, cosine = sin_cos(phi)
    sine_n, cosine_n = sin_cos(count * phi)
    still = phi == 0.0
    ratio = jnp.where(still, count, sine_n / jnp.where(still, 1.0, sine))
    cos_sum = ratio * (cosine_n * cosine + sine_n * sine)
    sin_sum = ratio * (sine_n * cosine - cosine_n * sine)
    return cos_sum, sin_sum


def gram(onset, omega_a, omega_b):
    count = onset.astype(F32)
    omega_a = jnp.full(count.shape, omega_a, F32)
    omega_b = jnp.full(count.shape, omega_b, F32)
    cos_aa, sin_aa = prefix_sums(omega_a, count)
    cos_bb, sin_bb = prefix_sums(omega_b, count)
    cos_sum, sin_sum = prefix_sums(0.5 * (omega_a + omega_b), count)
    cos_dif, sin_dif = prefix_sums(0.5 * (omega_a - omega_b), count)
    scale = 1.0 / NT
    g = {}
    g[0, 0] = scale * (count + cos_aa)
    g[1, 1] = scale * (count - cos_aa)
    g[0, 1] = -scale * sin_aa
    g[2, 2] = scale * (count + cos_bb)
    g[3, 3] = scale * (count - cos_bb)
    g[2, 3] = -scale * sin_bb
    g[0, 2] = scale * (cos_dif + cos_sum)
    g[1, 3] = scale * (cos_dif - cos_sum)
    g[0, 3] = -scale * (sin_sum - sin_dif)
    g[1, 2] = -scale * (sin_sum + sin_dif)
    for m in range(4):
        for n in range(m):
            g[m, n] = g[n, m]
    return g


def apply_gram(g, y):
    return [
        g[m, 0] * y[0] + g[m, 1] * y[1] + g[m, 2] * y[2] + g[m, 3] * y[3] for m in range(4)
    ]


def kernel(
    n_row, n_col,
    start_hbm, u_hbm, v_hbm, rank_ref, onset_r_hbm, onset_s_hbm, omega_hbm,
    out_ref,
    start_buf, u_buf, v_buf, omega_ref, onset_r_buf, onset_s_buf, local_sem,
    send1, recv1, send2, recv2, send3, recv3, send4, recv4,
    ssem1, rsem1, ssem2, rsem2, ssem3, rsem3, ssem4, rsem4,
):
    row = lax.axis_index("trow")
    col = lax.axis_index("tcol")
    freq = lax.axis_index("tm")
    group_r, group_s = 2 * n_col, 2 * n_row
    me_r = col * 2 + freq
    me_s = row * 2 + freq
    half_s = recv3.shape[2]
    half_r = u_buf.shape[1] // 2

    def peer_r(index):
        return {"tcol": index // 2, "tm": index % 2}

    def peer_s(index):
        return {"trow": index // 2, "tm": index % 2}

    onset_r_src = onset_r_hbm.at[:, pl.ds(pl.multiple_of(freq * half_r, half_r), half_r)]
    onset_s_src = onset_s_hbm.at[:, pl.ds(pl.multiple_of(freq * half_s, half_s), half_s)]
    moves = [
        (start_hbm.at[0], start_buf),
        (v_hbm.at[0, 0], v_buf.at[0]),
        (v_hbm.at[0, 1], v_buf.at[1]),
        (u_hbm.at[0, 0, pl.ds(0, half_r)], u_buf.at[0, pl.ds(0, half_r)]),
        (u_hbm.at[0, 1, pl.ds(0, half_r)], u_buf.at[1, pl.ds(0, half_r)]),
        (u_hbm.at[0, 0, pl.ds(half_r, half_r)], u_buf.at[0, pl.ds(half_r, half_r)]),
        (u_hbm.at[0, 1, pl.ds(half_r, half_r)], u_buf.at[1, pl.ds(half_r, half_r)]),
        (omega_hbm, omega_ref),
        (onset_r_src, onset_r_buf),
        (onset_s_src, onset_s_buf),
    ]
    copies = [
        pltpu.make_async_copy(source, target, local_sem.at[place])
        for place, (source, target) in enumerate(moves)
    ]
    for copy in copies:
        copy.start()

    barrier = pltpu.get_barrier_semaphore()
    for step in range(1, group_r):
        pl.semaphore_signal(
            barrier, inc=1, device_id=peer_r((me_r + step) % group_r), device_id_type=MESH
        )
    for step in range(1, group_s):
        pl.semaphore_signal(
            barrier, inc=1, device_id=peer_s((me_s + step) % group_s), device_id_type=MESH
        )

    def remote(source, target, ssem, rsem, device):
        return pltpu.make_async_remote_copy(
            src_ref=source, dst_ref=target, send_sem=ssem, recv_sem=rsem,
            device_id=device, device_id_type=MESH,
        )

    sent = []

    def push(send_of, recv, ssem, rsem, me, index, peer):
        copy = remote(send_of(index), recv.at[me], ssem.at[index], rsem.at[me], peer(index))
        copy.start()
        sent.append(copy)

    def arrivals(send_of, recv, ssem, rsem, me, group, peer):
        for step in range(1, group):
            index = (me + step) % group
            remote(
                send_of(index), recv.at[index], ssem.at[index], rsem.at[index], peer(index)
            ).wait_recv()

    def window(recv, group, onset):
        parts = []
        for k in range(2):
            total = recv[k].astype(F32)
            for other in range(1, group // 2):
                total = total + recv[2 * other + k].astype(F32)
            parts += [total[:8], total[8:]]
        done = apply_gram(onset, parts)
        return [
            jnp.concatenate([done[2 * k], done[2 * k + 1]], axis=0).astype(BF16)
            for k in range(2)
        ]

    of1 = lambda index: send1.at[index % 2]
    of3 = lambda index: send3.at[index % 2]

    copies[0].wait()
    rows_in = jnp.concatenate([start_buf[0], start_buf[1]], axis=0).astype(BF16)
    copies[1].wait()
    first_real = contract_last(rows_in, v_buf[0])
    copies[2].wait()
    first_imag = contract_last(rows_in, v_buf[1])
    lane = lax.broadcasted_iota(jnp.int32, (8, first_real.shape[1]), 1)
    keep = lane < rank_ref[0, 0, 0] * RBLK
    t_real = jnp.where(keep, first_real[:8] - first_imag[8:], 0.0)
    t_imag = jnp.where(keep, first_imag[:8] + first_real[8:], 0.0)
    packed = jnp.concatenate([t_real, t_imag], axis=0).astype(BF16)

    for half in range(2):
        rows = pl.ds(half * half_r, half_r)
        copies[3 + 2 * half].wait()
        second_real = contract_last(packed, u_buf[0, rows])
        copies[4 + 2 * half].wait()
        second_imag = contract_last(packed, u_buf[1, rows])
        send1[half] = jnp.concatenate(
            [second_real[:8] - second_imag[8:], second_imag[:8] + second_real[8:]], axis=0
        ).astype(BF16)
        if half == 0:
            pl.semaphore_wait(barrier, group_r + group_s - 2)
        for step in range(1, n_col):
            push(
                of1, recv1, ssem1, rsem1, me_r, ((col + step) % n_col) * 2 + half, peer_r
            )
    push(of1, recv1, ssem1, rsem1, me_r, me_r + 1 - 2 * freq, peer_r)
    recv1[me_r] = send1[freq]
    for place in (7, 8, 9):
        copies[place].wait()
    gram_r = gram(onset_r_buf[...], omega_ref[0], omega_ref[1])

    arrivals(of1, recv1, ssem1, rsem1, me_r, group_r, peer_r)
    done = window(recv1, group_r, gram_r)
    for k in range(2):
        send2[k] = done[k]
    middle = remote(send2.at[1 - freq], recv2.at[freq], ssem2, rsem2, {"tm": 1 - freq})
    middle.start()
    recv2[freq] = send2[freq]
    gram_s = gram(onset_s_buf[...], omega_ref[0], omega_ref[1])
    remote(send2.at[freq], recv2.at[1 - freq], ssem2, rsem2, {"tm": 1 - freq}).wait_recv()
    rows_back = jnp.concatenate([recv2[0], recv2[1]], axis=1)

    first_real = contract_inner(rows_back, u_buf[0])
    first_imag = contract_inner(rows_back, u_buf[1])
    s_real = jnp.where(keep, first_real[:8] + first_imag[8:], 0.0)
    s_imag = jnp.where(keep, first_real[8:] - first_imag[:8], 0.0)
    packed_back = jnp.concatenate([s_real, s_imag], axis=0).astype(BF16)
    for half in range(2):
        span = slice(half * half_s, (half + 1) * half_s)
        second_real = contract_inner(packed_back, v_buf[0, :, span])
        second_imag = contract_inner(packed_back, v_buf[1, :, span])
        send3[half] = jnp.concatenate(
            [second_real[:8] + second_imag[8:], second_real[8:] - second_imag[:8]], axis=0
        ).astype(BF16)
        for step in range(1, n_row):
            push(
                of3, recv3, ssem3, rsem3, me_s, ((row + step) % n_row) * 2 + half, peer_s
            )
    partner = me_s + 1 - 2 * freq
    push(of3, recv3, ssem3, rsem3, me_s, partner, peer_s)
    recv3[me_s] = send3[freq]
    out_ref[1, 0] = rows_back[:8]
    out_ref[1, 1] = rows_back[8:]
    arrivals(of3, recv3, ssem3, rsem3, me_s, group_s, peer_s)
    done = window(recv3, group_s, gram_s)
    for k in range(2):
        send4[k] = done[k]
    last = remote(send4.at[1 - freq], recv4.at[freq], ssem4, rsem4, {"tm": 1 - freq})
    last.start()
    recv4[freq] = send4[freq]
    remote(send4.at[freq], recv4.at[1 - freq], ssem4, rsem4, {"tm": 1 - freq}).wait_recv()
    back = jnp.concatenate([recv4[0], recv4[1]], axis=1)
    out_ref[0, 0] = back[:8]
    out_ref[0, 1] = back[8:]
    for copy in sent:
        copy.wait_send()
    middle.wait_send()
    last.wait_send()


def per_device(start_field, u_tiles, v_tiles, rank_blocks, onset_receiver, onset_source, omega):
    n_row = lax.axis_size("trow")
    n_col = lax.axis_size("tcol")
    group_r, group_s = 2 * n_col, 2 * n_row
    tile_r, tile_s = u_tiles.shape[2], v_tiles.shape[3]
    half_r, half_s = tile_r // 2, tile_s // 2
    hbm = pl.BlockSpec(memory_space=pl.ANY)
    piece_r = lambda count: pltpu.VMEM((count, 16, half_r), BF16)
    piece_s = lambda count: pltpu.VMEM((count, 16, half_s), BF16)
    sems = pltpu.SemaphoreType.DMA
    fields = pl.pallas_call(
        functools.partial(kernel, n_row, n_col),
        out_shape=jax.ShapeDtypeStruct((2, 2, 8, tile_r), BF16),
        in_specs=[hbm] * 3 + [pl.BlockSpec(memory_space=pltpu.SMEM)] + [hbm] * 3,
        out_specs=pl.BlockSpec(memory_space=pltpu.VMEM),
        scratch_shapes=[
            pltpu.VMEM(start_field.shape[1:], F32),
            pltpu.VMEM(u_tiles.shape[1:], BF16),
            pltpu.VMEM(v_tiles.shape[1:], BF16),
            pltpu.SMEM((2,), F32),
            pltpu.VMEM((8, half_r), jnp.int32),
            pltpu.VMEM((8, half_s), jnp.int32),
            sems((10,)),
            piece_r(2), piece_r(group_r), piece_r(2), piece_r(2),
            piece_s(2), piece_s(group_s), piece_s(2), piece_s(2),
        ]
        + [sems((group_r,))] * 2
        + [sems(())] * 2
        + [sems((group_s,))] * 2
        + [sems(())] * 2,
        compiler_params=pltpu.CompilerParams(
            collective_id=0, has_side_effects=True, vmem_limit_bytes=24 * 1024 * 1024
        ),
    )(
        pin(start_field), pin(u_tiles), pin(v_tiles), rank_blocks,
        pin(onset_receiver), pin(onset_source), pin(omega),
    )
    return start_field - fields[:1].astype(F32), fields[1:]


def pin(x):
    return pltpu.with_memory_space_constraint(x, pltpu.MemorySpace.HBM)


def solution(mesh):
    placed = (
        P("tm", None, None, "tcol"),
        P("tm", None, "trow", "tcol"),
        P("tm", None, "trow", "tcol"),
        P("tm", "trow", "tcol"),
        P(None, "trow"),
        P(None, "tcol"),
        P(),
    )
    return jax.shard_map(
        per_device,
        mesh=mesh,
        in_specs=placed,
        out_specs=(P("tm", None, None, "tcol"), P("tm", None, None, "trow")),
        check_vma=False,
    )
```

```python
import functools

import jax
import jax.numpy as jnp
from jax import lax
from jax.experimental import pallas as pl
from jax.experimental.pallas import tpu as pltpu
from jax.sharding import PartitionSpec as P

RBLK = 256
NT = 1024
MESH = pl.DeviceIdType.MESH
F32 = jnp.float32
BF16 = jnp.bfloat16


def contract_last(left_side, right_side):
    return lax.dot_general(
        left_side, right_side, (((1,), (1,)), ((), ())), preferred_element_type=F32
    )


def contract_inner(left_side, right_side):
    return lax.dot_general(
        left_side, right_side, (((1,), (0,)), ((), ())), preferred_element_type=F32
    )


def sin_cos(angle):
    turns = jnp.floor(angle * 0.6366197723675814 + 0.5)
    rest = angle - turns * 1.5703125
    rest = rest - turns * 4.837512969970703e-4
    rest = rest - turns * 7.549789948768648e-8
    square = rest * rest
    sine = rest + rest * square * (
        -1.6666654611e-1 + square * (8.3321608736e-3 - square * 1.9515295891e-4)
    )
    cosine = 1.0 - 0.5 * square + square * square * (
        4.166664568298827e-2 + square * (-1.388731625493765e-3 + square * 2.443315711809948e-5)
    )
    quarter = turns - 4.0 * jnp.floor(turns * 0.25)
    swap = (quarter == 1.0) | (quarter == 3.0)
    first = jnp.where(swap, cosine, sine)
    second = jnp.where(swap, sine, cosine)
    first = jnp.where(quarter >= 2.0, -first, first)
    second = jnp.where((quarter == 1.0) | (quarter == 2.0), -second, second)
    return first, second


def prefix_sums(phi, count):
    sine, cosine = sin_cos(phi)
    sine_n, cosine_n = sin_cos(count * phi)
    still = phi == 0.0
    ratio = jnp.where(still, count, sine_n / jnp.where(still, 1.0, sine))
    cos_sum = ratio * (cosine_n * cosine + sine_n * sine)
    sin_sum = ratio * (sine_n * cosine - cosine_n * sine)
    return cos_sum, sin_sum


def gram(onset, omega_a, omega_b):
    count = onset.astype(F32)
    omega_a = jnp.full(count.shape, omega_a, F32)
    omega_b = jnp.full(count.shape, omega_b, F32)
    cos_aa, sin_aa = prefix_sums(omega_a, count)
    cos_bb, sin_bb = prefix_sums(omega_b, count)
    cos_sum, sin_sum = prefix_sums(0.5 * (omega_a + omega_b), count)
    cos_dif, sin_dif = prefix_sums(0.5 * (omega_a - omega_b), count)
    scale = 1.0 / NT
    g = {}
    g[0, 0] = scale * (count + cos_aa)
    g[1, 1] = scale * (count - cos_aa)
    g[0, 1] = -scale * sin_aa
    g[2, 2] = scale * (count + cos_bb)
    g[3, 3] = scale * (count - cos_bb)
    g[2, 3] = -scale * sin_bb
    g[0, 2] = scale * (cos_dif + cos_sum)
    g[1, 3] = scale * (cos_dif - cos_sum)
    g[0, 3] = -scale * (sin_sum - sin_dif)
    g[1, 2] = -scale * (sin_sum + sin_dif)
    for m in range(4):
        for n in range(m):
            g[m, n] = g[n, m]
    return g


def apply_gram(g, y):
    return [
        g[m, 0] * y[0] + g[m, 1] * y[1] + g[m, 2] * y[2] + g[m, 3] * y[3] for m in range(4)
    ]


def kernel(
    n_row, n_col,
    start_hbm, u_hbm, v_hbm, rank_ref, onset_r_hbm, onset_s_hbm, omega_hbm,
    out_ref,
    start_buf, u_buf, v_buf, omega_ref, onset_r_buf, onset_s_buf, local_sem,
    send1, recv1, send2, recv2, send3, recv3, send4, recv4,
    ssem1, rsem1, ssem2, rsem2, ssem3, rsem3, ssem4, rsem4,
):
    row = lax.axis_index("trow")
    col = lax.axis_index("tcol")
    freq = lax.axis_index("tm")
    group_r, group_s = 2 * n_col, 2 * n_row
    me_r = col * 2 + freq
    me_s = row * 2 + freq
    half_s = recv3.shape[2]
    half_r = u_buf.shape[1] // 2

    def peer_r(index):
        return {"tcol": index // 2, "tm": index % 2}

    def peer_s(index):
        return {"trow": index // 2, "tm": index % 2}

    onset_r_src = onset_r_hbm.at[:, pl.ds(pl.multiple_of(freq * half_r, half_r), half_r)]
    onset_s_src = onset_s_hbm.at[:, pl.ds(pl.multiple_of(freq * half_s, half_s), half_s)]
    moves = [
        (start_hbm.at[0], start_buf),
        (v_hbm.at[0, 0], v_buf.at[0]),
        (v_hbm.at[0, 1], v_buf.at[1]),
        (u_hbm.at[0, 0, pl.ds(0, half_r)], u_buf.at[0, pl.ds(0, half_r)]),
        (u_hbm.at[0, 1, pl.ds(0, half_r)], u_buf.at[1, pl.ds(0, half_r)]),
        (u_hbm.at[0, 0, pl.ds(half_r, half_r)], u_buf.at[0, pl.ds(half_r, half_r)]),
        (u_hbm.at[0, 1, pl.ds(half_r, half_r)], u_buf.at[1, pl.ds(half_r, half_r)]),
        (omega_hbm, omega_ref),
        (onset_r_src, onset_r_buf),
        (onset_s_src, onset_s_buf),
    ]
    copies = [
        pltpu.make_async_copy(source, target, local_sem.at[place])
        for place, (source, target) in enumerate(moves)
    ]
    for copy in copies:
        copy.start()

    barrier = pltpu.get_barrier_semaphore()
    for step in range(1, group_r):
        pl.semaphore_signal(
            barrier, inc=1, device_id=peer_r((me_r + step) % group_r), device_id_type=MESH
        )
    for step in range(1, group_s):
        pl.semaphore_signal(
            barrier, inc=1, device_id=peer_s((me_s + step) % group_s), device_id_type=MESH
        )

    def remote(source, target, ssem, rsem, device):
        return pltpu.make_async_remote_copy(
            src_ref=source, dst_ref=target, send_sem=ssem, recv_sem=rsem,
            device_id=device, device_id_type=MESH,
        )

    sent = []

    def push(send_of, recv, ssem, rsem, me, index, peer):
        copy = remote(send_of(index), recv.at[me], ssem.at[index], rsem.at[me], peer(index))
        copy.start()
        sent.append(copy)

    def arrivals(send_of, recv, ssem, rsem, me, group, peer):
        for step in range(1, group):
            index = (me + step) % group
            remote(
                send_of(index), recv.at[index], ssem.at[index], rsem.at[index], peer(index)
            ).wait_recv()

    def window(recv, group, onset):
        parts = []
        for k in range(2):
            total = recv[k].astype(F32)
            for other in range(1, group // 2):
                total = total + recv[2 * other + k].astype(F32)
            parts += [total[:8], total[8:]]
        done = apply_gram(onset, parts)
        return [
            jnp.concatenate([done[2 * k], done[2 * k + 1]], axis=0).astype(BF16)
            for k in range(2)
        ]

    of1 = lambda index: send1.at[index % 2]
    of3 = lambda index: send3.at[index % 2]

    copies[0].wait()
    rows_in = jnp.concatenate([start_buf[0], start_buf[1]], axis=0).astype(BF16)
    copies[1].wait()
    first_real = contract_last(rows_in, v_buf[0])
    copies[2].wait()
    first_imag = contract_last(rows_in, v_buf[1])
    lane = lax.broadcasted_iota(jnp.int32, (8, first_real.shape[1]), 1)
    keep = lane < rank_ref[0, 0, 0] * RBLK
    t_real = jnp.where(keep, first_real[:8] - first_imag[8:], 0.0)
    t_imag = jnp.where(keep, first_imag[:8] + first_real[8:], 0.0)
    packed = jnp.concatenate([t_real, t_imag], axis=0).astype(BF16)

    for half in range(2):
        rows = pl.ds(half * half_r, half_r)
        copies[3 + 2 * half].wait()
        second_real = contract_last(packed, u_buf[0, rows])
        copies[4 + 2 * half].wait()
        second_imag = contract_last(packed, u_buf[1, rows])
        send1[half] = jnp.concatenate(
            [second_real[:8] - second_imag[8:], second_imag[:8] + second_real[8:]], axis=0
        ).astype(BF16)
        if half == 0:
            pl.semaphore_wait(barrier, group_r + group_s - 2)
        for step in range(1, n_col):
            push(
                of1, recv1, ssem1, rsem1, me_r, ((col + step) % n_col) * 2 + half, peer_r
            )
    push(of1, recv1, ssem1, rsem1, me_r, me_r + 1 - 2 * freq, peer_r)
    recv1[me_r] = send1[freq]
    for place in (7, 8, 9):
        copies[place].wait()
    gram_r = gram(onset_r_buf[...], omega_ref[0], omega_ref[1])

    arrivals(of1, recv1, ssem1, rsem1, me_r, group_r, peer_r)
    done = window(recv1, group_r, gram_r)
    for k in range(2):
        send2[k] = done[k]
    middle = remote(send2.at[1 - freq], recv2.at[freq], ssem2, rsem2, {"tm": 1 - freq})
    middle.start()
    recv2[freq] = send2[freq]
    gram_s = gram(onset_s_buf[...], omega_ref[0], omega_ref[1])
    own_rows = pl.ds(pl.multiple_of(freq * half_r, half_r), half_r)
    other_rows = pl.ds(pl.multiple_of((1 - freq) * half_r, half_r), half_r)
    own = send2[freq]
    own_real = contract_inner(own, u_buf[0, own_rows])
    own_imag = contract_inner(own, u_buf[1, own_rows])
    remote(send2.at[freq], recv2.at[1 - freq], ssem2, rsem2, {"tm": 1 - freq}).wait_recv()
    rows_back = jnp.concatenate([recv2[0], recv2[1]], axis=1)

    other = recv2[1 - freq]
    first_real = own_real + contract_inner(other, u_buf[0, other_rows])
    first_imag = own_imag + contract_inner(other, u_buf[1, other_rows])
    s_real = jnp.where(keep, first_real[:8] + first_imag[8:], 0.0)
    s_imag = jnp.where(keep, first_real[8:] - first_imag[:8], 0.0)
    packed_back = jnp.concatenate([s_real, s_imag], axis=0).astype(BF16)
    for half in range(2):
        span = slice(half * half_s, (half + 1) * half_s)
        second_real = contract_inner(packed_back, v_buf[0, :, span])
        second_imag = contract_inner(packed_back, v_buf[1, :, span])
        send3[half] = jnp.concatenate(
            [second_real[:8] + second_imag[8:], second_real[8:] - second_imag[:8]], axis=0
        ).astype(BF16)
        for step in range(1, n_row):
            push(
                of3, recv3, ssem3, rsem3, me_s, ((row + step) % n_row) * 2 + half, peer_s
            )
    partner = me_s + 1 - 2 * freq
    push(of3, recv3, ssem3, rsem3, me_s, partner, peer_s)
    recv3[me_s] = send3[freq]
    out_ref[1, 0] = rows_back[:8]
    out_ref[1, 1] = rows_back[8:]
    arrivals(of3, recv3, ssem3, rsem3, me_s, group_s, peer_s)
    done = window(recv3, group_s, gram_s)
    for k in range(2):
        send4[k] = done[k]
    last = remote(send4.at[1 - freq], recv4.at[freq], ssem4, rsem4, {"tm": 1 - freq})
    last.start()
    recv4[freq] = send4[freq]
    remote(send4.at[freq], recv4.at[1 - freq], ssem4, rsem4, {"tm": 1 - freq}).wait_recv()
    back = jnp.concatenate([recv4[0], recv4[1]], axis=1)
    out_ref[0, 0] = back[:8]
    out_ref[0, 1] = back[8:]
    for copy in sent:
        copy.wait_send()
    middle.wait_send()
    last.wait_send()


def per_device(start_field, u_tiles, v_tiles, rank_blocks, onset_receiver, onset_source, omega):
    n_row = lax.axis_size("trow")
    n_col = lax.axis_size("tcol")
    group_r, group_s = 2 * n_col, 2 * n_row
    tile_r, tile_s = u_tiles.shape[2], v_tiles.shape[3]
    half_r, half_s = tile_r // 2, tile_s // 2
    hbm = pl.BlockSpec(memory_space=pl.ANY)
    piece_r = lambda count: pltpu.VMEM((count, 16, half_r), BF16)
    piece_s = lambda count: pltpu.VMEM((count, 16, half_s), BF16)
    sems = pltpu.SemaphoreType.DMA
    fields = pl.pallas_call(
        functools.partial(kernel, n_row, n_col),
        out_shape=jax.ShapeDtypeStruct((2, 2, 8, tile_r), BF16),
        in_specs=[hbm] * 3 + [pl.BlockSpec(memory_space=pltpu.SMEM)] + [hbm] * 3,
        out_specs=pl.BlockSpec(memory_space=pltpu.VMEM),
        scratch_shapes=[
            pltpu.VMEM(start_field.shape[1:], F32),
            pltpu.VMEM(u_tiles.shape[1:], BF16),
            pltpu.VMEM(v_tiles.shape[1:], BF16),
            pltpu.SMEM((2,), F32),
            pltpu.VMEM((8, half_r), jnp.int32),
            pltpu.VMEM((8, half_s), jnp.int32),
            sems((10,)),
            piece_r(2), piece_r(group_r), piece_r(2), piece_r(2),
            piece_s(2), piece_s(group_s), piece_s(2), piece_s(2),
        ]
        + [sems((group_r,))] * 2
        + [sems(())] * 2
        + [sems((group_s,))] * 2
        + [sems(())] * 2,
        compiler_params=pltpu.CompilerParams(
            collective_id=0, has_side_effects=True, vmem_limit_bytes=24 * 1024 * 1024
        ),
    )(
        pin(start_field), pin(u_tiles), pin(v_tiles), rank_blocks,
        pin(onset_receiver), pin(onset_source), pin(omega),
    )
    return start_field - fields[:1].astype(F32), fields[1:]


def pin(x):
    return pltpu.with_memory_space_constraint(x, pltpu.MemorySpace.HBM)


def solution(mesh):
    placed = (
        P("tm", None, None, "tcol"),
        P("tm", None, "trow", "tcol"),
        P("tm", None, "trow", "tcol"),
        P("tm", "trow", "tcol"),
        P(None, "trow"),
        P(None, "tcol"),
        P(),
    )
    return jax.shard_map(
        per_device,
        mesh=mesh,
        in_specs=placed,
        out_specs=(P("tm", None, None, "tcol"), P("tm", None, None, "trow")),
        check_vma=False,
    )
```
